256 devices in a mesh: section: 16 (over y_hi, z), mp: 16 (over y_lo, x, core).
Axes of the slice: x: 4, y: 4 (y_hi: 2, y_lo: 2; y = y_hi * 2 + y_lo), z: 8, core: 2. Of those that a mesh axis runs over, the one named last changes fastest.
Arguments:
- pixels: bfloat16 [2048, 12, 256], P('mp')
- band_pick: int32 [16, 4], replicated, may hold values from 0 to 11, as said below
- band_count: int32 [16], replicated, may hold values from 1 to 4, as said below
- tok_gain: float32 [16, 7168], P(None, 'mp'), may hold values from 0.1 to 1.9
- bands_weight: bfloat16 [12, 256, 7168], P(None, None, 'mp')
- plan: int32 [4], replicated, may hold values from 0 to 3, each once
- trunk_gain: float32 [7168], replicated, may hold values from 0.1 to 1.9
- query_weight: bfloat16 [7168, 7168], P(None, 'mp'), may hold values from -0.0625 to 0.0625
- query_cot: bfloat16 [2048, 7168], P('section', 'mp'), may hold values from -6 to 6
- resid_cot: bfloat16 [2048, 7168], P('section', 'mp'), may hold values from -1.5 to 1.5
Outputs:
- queries: bfloat16 [2048, 7168], P('section', 'mp')
- band_grads: bfloat16 [12, 256, 7168], P(None, 'section', 'mp')
The draws below stay inside these ranges and needn't reach their ends.
Inputs may be any that keep to these rules, and one draw needn't show every extreme that they name: Each row of band_pick names 4 different bands. Group g reads the first band_count[g] slots of its row; some group reads 4 bands and some group one.
All inputs are finite; a program needn't handle non-finite values.
Results may differ from the reference program's by a relative error of at most 0.0058.
Values may be sent and summed in bfloat16 or wider, within the bound.
A program may use at most 128 MiB of HBM per device.

```python
import math
import jax
import jax.numpy as jnp
from jax import lax

D = 7168
BANDS = 12
PATCH = 256
SLOTS = 4
MICRO = 4
GROUPS = 16
NTOK = 2048
MICRO_TOK = 512


def draw_pixels(key, part):
    scale_key, value_key = jax.random.split(key)
    token_scale = jnp.exp(jax.random.uniform(scale_key, (NTOK, 1, 1), minval=0.0, maxval=math.log(10.0)))
    values = jax.random.normal(value_key, (NTOK, BANDS, PATCH))
    return (values * token_scale).astype(jnp.bfloat16)


def draw_bands_weight(key, part):
    spread_key, value_key = jax.random.split(key)
    column = jnp.arange(D, dtype=jnp.float32) / D
    spread = jnp.exp(jax.random.uniform(spread_key, (1, 1, D), minval=0.0, maxval=math.log(10.0)))
    rising = jnp.exp(math.log(3.0) * column)[None, None, :]
    values = jax.random.normal(value_key, (BANDS, PATCH, D))
    return (values * spread * rising / (3.0 * math.sqrt(PATCH))).astype(jnp.bfloat16)


def draw_band_pick(key, part):
    group_keys = jax.random.split(key, GROUPS)
    picks = jax.vmap(lambda each_key: jax.random.permutation(each_key, BANDS)[:SLOTS])(group_keys)
    return picks.astype(jnp.int32)


def draw_band_count(key, part):
    count_key, order_key = jax.random.split(key)
    counts = jax.random.randint(count_key, (GROUPS,), 1, SLOTS + 1)
    ranking = jax.random.permutation(order_key, GROUPS)
    counts = jnp.where(ranking == 0, SLOTS, jnp.where(ranking == 1, 1, counts))
    return counts.astype(jnp.int32)


def block_scale(stream_key, shape, cuts, low, top_value):
    factor_of = 1.0
    for axis_at, shards_of in cuts:
        draws = jax.random.uniform(jax.random.fold_in(jax.random.fold_in(stream_key, 6), axis_at), (shards_of,), jnp.float32, low / len(cuts), top_value / len(cuts))
        factor_of = factor_of * jnp.repeat(jnp.exp(draws), shape[axis_at] // shards_of).reshape((-1,) + (1,) * (len(shape) - 1 - axis_at))
    return factor_of


def centred(own_key, shape, width, limit, pieces=(), kind=jnp.bfloat16):
    array = jax.random.normal(own_key, shape, jnp.float32) * width
    if len(pieces) > 0:
        array = block_scale(own_key, shape, pieces, -0.22, 0.18) * array
    return jnp.clip(array, min=-limit, max=limit).astype(kind)


def setup_inputs(seed: int = 0) -> dict:
    streams_of = jax.random.split(jax.random.key(seed), 11)
    return {
        "pixels": draw_pixels(jax.random.fold_in(streams_of[10], 71), 0),
        "band_pick": draw_band_pick(jax.random.fold_in(streams_of[10], 71), 0),
        "band_count": draw_band_count(jax.random.fold_in(streams_of[10], 71), 0),
        "tok_gain": jnp.clip(1.0 + 0.18 * jax.random.normal(streams_of[3], (GROUPS, D), jnp.float32), 0.1, 1.9),
        "bands_weight": draw_bands_weight(jax.random.fold_in(streams_of[10], 71), 0),
        "plan": jax.random.permutation(streams_of[5], MICRO).astype(jnp.int32),
        "trunk_gain": jnp.clip(1.0 + 0.18 * jax.random.normal(streams_of[6], (D,), jnp.float32), 0.1, 1.9),
        "query_weight": centred(streams_of[7], (D, D), D ** -0.5, 0.0625, ((1, 16),)),
        "query_cot": centred(streams_of[8], (NTOK, D), 1.0, 6.0, ((0, 16), (1, 16))),
        "resid_cot": centred(streams_of[9], (NTOK, D), 0.25, 1.5, ((0, 16), (1, 16))),
    }


EPSILON = 1e-05

def group_terms(pixels, picked, used_count, bands_weight):
    live_slots = (jnp.arange(SLOTS) < used_count).astype(pixels.dtype)
    chosen = pixels[:, picked, :] * live_slots[None, :, None]
    flat_pixels = chosen.reshape(NTOK, SLOTS * PATCH)
    slot_weights = bands_weight[picked].reshape(SLOTS * PATCH, D)
    group_out = jnp.dot(flat_pixels, slot_weights, preferred_element_type=jnp.float32)
    group_scale = lax.rsqrt(lax.optimization_barrier(jnp.mean(group_out * group_out, axis=1)) + EPSILON)
    return (flat_pixels, group_out, group_scale)

def reference(pixels, band_pick, band_count, tok_gain, bands_weight, plan, trunk_gain, query_weight, query_cot, resid_cot):

    def forward_group(running, group_data):
        picked, used_count, gain_row = group_data
        flat_pixels, group_out, group_scale = group_terms(pixels, picked, used_count, bands_weight)
        return (running + group_out * group_scale[:, None] * gain_row[None, :], None)
    embed, _ = lax.scan(forward_group, jnp.zeros((NTOK, D), jnp.float32), (band_pick, band_count, tok_gain))
    reordered = embed.reshape(MICRO, MICRO_TOK, D)[plan].reshape(NTOK, D)
    trunk_low = lax.optimization_barrier(reordered.astype(jnp.bfloat16))
    trunk_in = trunk_low.astype(jnp.float32)
    row_scale = lax.rsqrt(lax.optimization_barrier(jnp.mean(trunk_in * trunk_in, axis=1)) + EPSILON)
    normed = (trunk_in * row_scale[:, None] * trunk_gain[None, :]).astype(jnp.bfloat16)
    queries = jnp.dot(normed, query_weight, preferred_element_type=jnp.float32).astype(jnp.bfloat16)
    normed_grad = jnp.dot(query_cot, query_weight.T, preferred_element_type=jnp.float32)
    row_stat = lax.optimization_barrier(jnp.mean(trunk_in * trunk_gain[None, :] * normed_grad, axis=1))
    norm_grad = row_scale[:, None] * trunk_gain[None, :] * normed_grad - trunk_in * (row_scale ** 3)[:, None] * row_stat[:, None]
    input_grad = lax.optimization_barrier((resid_cot.astype(jnp.float32) + norm_grad).astype(jnp.bfloat16))
    inverse = jnp.argsort(plan).astype(jnp.int32)
    embed_grad = input_grad.reshape(MICRO, MICRO_TOK, D)[inverse].reshape(NTOK, D).astype(jnp.float32)

    def backward_group(running, group_data):
        picked, used_count, gain_row = group_data
        flat_pixels, group_out, group_scale = group_terms(pixels, picked, used_count, bands_weight)
        unit_grad = embed_grad * gain_row[None, :]
        group_stat = lax.optimization_barrier(jnp.mean(group_out * unit_grad, axis=1))
        group_grad = (group_scale[:, None] * unit_grad - group_out * (group_scale ** 3)[:, None] * group_stat[:, None]).astype(jnp.bfloat16)
        slot_grads = jnp.dot(flat_pixels.T, group_grad, preferred_element_type=jnp.float32).reshape(SLOTS, PATCH, D)
        return (running.at[picked].add(slot_grads), None)
    band_grads, _ = lax.scan(backward_group, jnp.zeros((BANDS, PATCH, D), jnp.float32), (band_pick, band_count, tok_gain))
    return (queries, band_grads.astype(jnp.bfloat16))
```

```python
import functools

import jax
import jax.numpy as jnp
from jax import lax
from jax.experimental import pallas as pl
from jax.experimental.pallas import tpu as pltpu
from jax.sharding import PartitionSpec as P

EPSILON = 1e-05
MESH = pl.DeviceIdType.MESH
F32 = jnp.float32
BF16 = jnp.bfloat16
NEAR = 8
TILE = 16


def kernel(
    model_width,
    pick_ref,
    count_ref,
    plan_ref,
    pix_ref,
    gain_ref,
    tg_ref,
    qc_ref,
    rc_ref,
    w_hbm,
    wq_hbm,
    q_ref,
    bg_ref,
    live,
    member,
    w_ref,
    wq_ref,
    cand,
    xg,
    stage,
    crecv,
    p_ref,
    go,
    sums,
    table,
    ps1,
    ps2,
    ag,
    tgng,
    gb,
    pb,
    cr,
    ybuf,
    yrecv,
    acc,
    local_sem,
    cand_send,
    cand_recv,
    x_send,
    x_recv,
    c_send,
    c_recv,
    p1_send,
    p1_recv,
    p2_send,
    p2_recv,
    ag_send,
    ag_recv,
    cr_send,
    cr_recv,
    y_send,
    y_recv,
):
    groups, slots = pick_ref.shape
    bands = w_ref.shape[0]
    peers = xg.shape[0]
    tokens, cols = qc_ref.shape
    chunks = tokens // TILE
    me = lax.axis_index("mp")
    section = lax.axis_index("section")
    half = section // NEAR
    ring = lax.rem(section, NEAR)
    low = lax.rem(section, 4)
    block = section // 4

    copy_wq = pltpu.make_async_copy(wq_hbm, wq_ref, local_sem.at[0])
    copy_w = pltpu.make_async_copy(w_hbm, w_ref, local_sem.at[1])
    copy_wq.start()
    copy_w.start()

    def peer(i):
        return lax.rem(me + i, peers)

    def at_ring(step):
        return half * NEAR + lax.rem(ring + step + NEAR, NEAR)

    down, up = at_ring(-1), at_ring(1)
    across = (1 - half) * NEAR + ring

    barrier = pltpu.get_barrier_semaphore()

    @pl.loop(1, peers)
    def _(i):
        pl.semaphore_signal(barrier, inc=1, device_id={"mp": peer(i)}, device_id_type=MESH)

    for other in (down, up, across):
        pl.semaphore_signal(barrier, inc=1, device_id={"section": other}, device_id_type=MESH)
    pl.semaphore_wait(barrier, peers - 1 + 3)

    def cand_copy(i):
        to = peer(i)
        return pltpu.make_async_remote_copy(
            src_ref=pix_ref.at[to],
            dst_ref=cand.at[me // 4],
            send_sem=cand_send.at[i],
            recv_sem=cand_recv.at[me // 4],
            device_id={"mp": to},
            device_id_type=MESH,
        )

    owner = lax.rem(me, 4) == low
    own_piece = pltpu.make_async_copy(pix_ref.at[me], cand.at[me // 4], cand_recv.at[me // 4])

    @pl.when(owner)
    def _():
        own_piece.start()

        @pl.loop(1, peers)
        def _(i):
            cand_copy(i).start()

    table[...] = jnp.zeros_like(table)

    @pl.loop(0, groups)
    def _(g):
        used = count_ref[g]
        for k in range(slots):
            live[g, k] = jnp.where(k < used, 1.0, 0.0).astype(F32)
        for b in range(bands):
            hit = jnp.float32(0.0)
            for k in range(slots):
                same = jnp.logical_and(pick_ref[g, k] == b, k < used)
                hit = hit + jnp.where(same, 1.0, 0.0).astype(F32)
            member[g, b] = hit

    copy_wq.wait()

    @pl.loop(0, peers)
    def _(j):
        rows = pl.ds(pl.multiple_of(j * cols, 64), cols)
        stage[j] = lax.dot_general(
            qc_ref[...], wq_ref[rows, :], (((1,), (1,)), ((), ())), preferred_element_type=F32
        ).astype(BF16)

    for c in range(4):
        pltpu.make_async_copy(pix_ref.at[0], cand.at[c], cand_recv.at[c]).wait()

    xg[me] = cand[plan_ref[block]]

    def send_own(buf, send, recv):
        def at(i):
            return pltpu.make_async_remote_copy(
                src_ref=buf.at[me],
                dst_ref=buf.at[me],
                send_sem=send.at[i],
                recv_sem=recv.at[me],
                device_id={"mp": peer(i)},
                device_id_type=MESH,
            )

        @pl.loop(1, peers)
        def _(i):
            at(i).start()

    def wait_recv(buf, recv):
        @pl.loop(1, peers)
        def _(i):
            src = peer(i)
            pltpu.make_async_copy(buf.at[src], buf.at[src], recv.at[src]).wait()

    def wait_send(buf, send):
        @pl.loop(1, peers)
        def _(i):
            pltpu.make_async_copy(buf.at[me], buf.at[me], send.at[i]).wait()

    send_own(xg, x_send, x_recv)

    @pl.loop(1, peers)
    def _(i):
        to = peer(i)
        pltpu.make_async_remote_copy(
            src_ref=stage.at[to],
            dst_ref=crecv.at[me],
            send_sem=c_send.at[i],
            recv_sem=c_recv.at[me],
            device_id={"mp": to},
            device_id_type=MESH,
        ).start()

    crecv[me] = stage[me]
    copy_w.wait()
    wait_recv(xg, x_recv)

    half_bands = bands // 2

    def band_pixels(b):
        side = b // half_bands
        start = pl.multiple_of(lax.rem(b, half_bands) * TILE, TILE)
        return jnp.concatenate(
            [xg[2 * i + side, pl.ds(start, TILE), :] for i in range(peers // 2)], axis=0
        )

    @pl.loop(0, bands)
    def _(b):
        p_ref[b] = jnp.dot(band_pixels(b), w_ref[b], preferred_element_type=F32)

    lane = lax.broadcasted_iota(jnp.int32, (TILE, 128), 1)

    def put(stat, at, value):
        return jnp.where(lane == at, jnp.sum(value, axis=1, keepdims=True), stat)

    @pl.loop(0, chunks)
    def _(r):
        rows = pl.ds(pl.multiple_of(r * TILE, TILE), TILE)
        stat = jnp.zeros((TILE, 128), F32)
        resid = rc_ref[rows, :].astype(F32)
        for g in range(groups):
            out = live[g, 0] * p_ref[pick_ref[g, 0], rows, :]
            for k in range(1, slots):
                out = out + live[g, k] * p_ref[pick_ref[g, k], rows, :]
            go[g, rows, :] = out
            stat = put(stat, g, out * out)
            stat = put(stat, groups + g, out * gain_ref[g : g + 1, :] * resid)
        sums[rows, :] = stat

    ps1[me] = sums[...].T[: ps1.shape[1], :]
    send_own(ps1, p1_send, p1_recv)
    wait_recv(ps1, p1_recv)

    def total(buf):
        value = buf[0]
        for i in range(1, peers):
            value = value + buf[i]
        return value

    first = total(ps1)
    scale = lax.rsqrt(first[:groups] / model_width + EPSILON)
    table[0:groups, :] = scale
    sums[...] = table[...].T

    @pl.loop(0, chunks)
    def _(r):
        rows = pl.ds(pl.multiple_of(r * TILE, TILE), TILE)
        col = sums[rows, :]
        value = jnp.zeros((TILE, cols), F32)
        for g in range(groups):
            value = value + go[g, rows, :] * col[:, g : g + 1] * gain_ref[g : g + 1, :]
        ag[me, rows, :] = value.astype(BF16)

    wait_recv(crecv, c_recv)
    own_gain = tg_ref[pl.ds(me, 1), :]

    @pl.loop(0, chunks)
    def _(r):
        rows = pl.ds(pl.multiple_of(r * TILE, TILE), TILE)
        grad = crecv[0, rows, :].astype(F32)
        for i in range(1, peers):
            grad = grad + crecv[i, rows, :].astype(F32)
        grad = grad * own_gain
        tgng[rows, :] = grad
        trunk = ag[me, rows, :].astype(F32)
        stat = jnp.zeros((TILE, 128), F32)
        stat = put(stat, 2 * groups, trunk * trunk)
        stat = put(stat, 2 * groups + 1, trunk * grad)
        for g in range(groups):
            unit = go[g, rows, :] * gain_ref[g : g + 1, :]
            stat = put(stat, g, unit * grad)
            stat = put(stat, groups + g, unit * trunk)
        sums[rows, :] = stat

    ps2[me] = sums[...].T[: ps2.shape[1], :]
    send_own(ps2, p2_send, p2_recv)
    send_own(ag, ag_send, ag_recv)
    wait_recv(ps2, p2_recv)
    second = total(ps2)
    row_scale = lax.rsqrt(second[2 * groups : 2 * groups + 1] / model_width + EPSILON)
    row_stat = second[2 * groups + 1 : 2 * groups + 2] / model_width
    cube_stat = row_scale * row_scale * row_scale * row_stat
    group_stat = (
        first[groups : 2 * groups]
        + row_scale * second[:groups]
        - cube_stat * second[groups : 2 * groups]
    ) / model_width
    table[groups : 2 * groups, :] = scale * scale * scale * group_stat
    table[2 * groups : 2 * groups + 1, :] = row_scale
    table[2 * groups + 1 : 2 * groups + 2, :] = cube_stat
    sums[...] = table[...].T

    @pl.loop(0, chunks)
    def _(r):
        rows = pl.ds(pl.multiple_of(r * TILE, TILE), TILE)
        col = sums[rows, :]
        trunk = ag[me, rows, :].astype(F32)
        grad = (
            rc_ref[rows, :].astype(F32)
            + col[:, 2 * groups : 2 * groups + 1] * tgng[rows, :]
            - col[:, 2 * groups + 1 : 2 * groups + 2] * trunk
        )
        grad = grad.astype(BF16).astype(F32)
        for g in range(groups):
            go[g, rows, :] = (
                col[:, g : g + 1] * (grad * gain_ref[g : g + 1, :])
                - go[g, rows, :] * col[:, groups + g : groups + g + 1]
            )
        for b0 in range(0, bands, 3):
            found = [jnp.zeros((TILE, cols), F32) for _ in range(3)]
            for g in range(groups):
                value = go[g, rows, :]
                found = [found[d] + member[g, b0 + d] * value for d in range(3)]
            for d in range(3):
                gb[b0 + d, rows, :] = found[d].astype(BF16)

    @pl.loop(0, bands)
    def _(b):
        value = lax.dot_general(
            band_pixels(b), gb[b], (((0,), (0,)), ((), ())), preferred_element_type=F32
        )
        rows = pl.ds(pl.multiple_of(b * TILE, TILE), TILE)
        pb[:, rows, :] = value.reshape(pb.shape[0], TILE, cols).astype(BF16)

    def unit(way, h, t):
        offset = (4 - t) if way else (t - 4)
        return h * NEAR + lax.rem(ring + offset + NEAR, NEAR)

    def link(way, h, t):
        return pltpu.make_async_remote_copy(
            src_ref=pb.at[unit(way, h, t)],
            dst_ref=cr.at[way, h, t],
            send_sem=cr_send.at[way, h, t],
            recv_sem=cr_recv.at[way, h, t],
            device_id={"section": up if way else down},
            device_id_type=MESH,
        )

    for way, h, t in ((0, 0, 0), (1, 1, 0), (0, 1, 1), (1, 0, 1)):
        link(way, h, t).start()

    def advance(way, h, t):
        link(way, h, t - 1).wait_recv()
        at = unit(way, h, t)
        pb[at] = (pb[at].astype(F32) + cr[way, h, t - 1].astype(F32)).astype(BF16)
        link(way, h, t).start()

    advance(0, 0, 1)
    advance(1, 1, 1)
    advance(0, 1, 2)
    advance(1, 0, 2)

    wait_recv(ag, ag_recv)
    acc[...] = jnp.zeros_like(acc)
    scale_col = sums[:, 2 * groups : 2 * groups + 1]

    @pl.loop(0, peers)
    def _(j):
        rows = pl.ds(pl.multiple_of(j * cols, 64), cols)
        normed = (ag[j].astype(F32) * scale_col * tg_ref[pl.ds(j, 1), :]).astype(BF16)
        acc[...] += jnp.dot(normed, wq_ref[rows, :], preferred_element_type=F32)

    q_ref[...] = acc[...].astype(BF16)

    advance(0, 0, 2)
    advance(1, 1, 2)
    advance(0, 1, 3)
    advance(1, 0, 3)
    advance(0, 0, 3)
    advance(1, 1, 3)
    for way, h in ((0, 1), (1, 0), (0, 0), (1, 1)):
        link(way, h, 3).wait_recv()

    def gathered(h):
        return (
            pb[h * NEAR + ring].astype(F32)
            + cr[0, h, 3].astype(F32)
            + cr[1, h, 3].astype(F32)
        )

    ybuf[...] = gathered(1 - half).astype(BF16)
    over = pltpu.make_async_remote_copy(
        src_ref=ybuf,
        dst_ref=yrecv,
        send_sem=y_send,
        recv_sem=y_recv,
        device_id={"section": across},
        device_id_type=MESH,
    )
    over.start()
    over.wait_recv()
    bg_ref[...] = (gathered(half) + yrecv[...].astype(F32)).astype(BF16)

    over.wait_send()
    for way, h, t0 in ((0, 0, 0), (1, 1, 0), (0, 1, 1), (1, 0, 1)):
        for t in range(t0, 4):
            link(way, h, t).wait_send()

    @pl.when(owner)
    def _():
        @pl.loop(1, peers)
        def _(i):
            cand_copy(i).wait_send()

    wait_send(xg, x_send)
    wait_send(crecv, c_send)
    wait_send(ps1, p1_send)
    wait_send(ps2, p2_send)
    wait_send(ag, ag_send)


def body(
    pixels,
    band_pick,
    band_count,
    tok_gain,
    bands_weight,
    plan,
    trunk_gain,
    query_weight,
    query_cot,
    resid_cot,
):
    peers = lax.axis_size("mp")
    sections = lax.axis_size("section")
    groups = band_pick.shape[0]
    tokens, bands, patch = pixels.shape
    cols = bands_weight.shape[2]
    model_width = cols * peers
    piece = tokens * bands // peers
    pieces = (
        pixels.reshape(tokens // TILE, TILE, bands, patch)
        .transpose(0, 2, 1, 3)
        .reshape(peers, piece, patch)
    )
    rows = bands * patch // sections
    vmem = pl.BlockSpec(memory_space=pltpu.VMEM)
    smem = pl.BlockSpec(memory_space=pltpu.SMEM)
    hbm = pl.BlockSpec(memory_space=pl.ANY)
    dma = pltpu.SemaphoreType.DMA
    queries, grads = pl.pallas_call(
        functools.partial(kernel, model_width),
        out_shape=(
            jax.ShapeDtypeStruct((tokens, cols), BF16),
            jax.ShapeDtypeStruct((rows, cols), BF16),
        ),
        in_specs=[smem] * 3 + [vmem] * 5 + [hbm] * 2,
        out_specs=(vmem, vmem),
        scratch_shapes=[
            pltpu.SMEM((groups, band_pick.shape[1]), F32),
            pltpu.SMEM((groups, bands), F32),
            pltpu.VMEM(bands_weight.shape, BF16),
            pltpu.VMEM(query_weight.shape, BF16),
            pltpu.VMEM((4, piece, patch), BF16),
            pltpu.VMEM((peers, piece, patch), BF16),
            pltpu.VMEM((peers, tokens, cols), BF16),
            pltpu.VMEM((peers, tokens, cols), BF16),
            pltpu.VMEM((bands, tokens, cols), F32),
            pltpu.VMEM((groups, tokens, cols), F32),
            pltpu.VMEM((tokens, 128), F32),
            pltpu.VMEM((128, tokens), F32),
            pltpu.VMEM((peers, 2 * groups, tokens), F32),
            pltpu.VMEM((peers, 2 * groups + 8, tokens), F32),
            pltpu.VMEM((peers, tokens, cols), BF16),
            pltpu.VMEM((tokens, cols), F32),
            pltpu.VMEM((bands, tokens, cols), BF16),
            pltpu.VMEM((sections, rows, cols), BF16),
            pltpu.VMEM((2, 2, 4, rows, cols), BF16),
            pltpu.VMEM((rows, cols), BF16),
            pltpu.VMEM((rows, cols), BF16),
            pltpu.VMEM((tokens, cols), F32),
            dma((2,)),
            dma((peers,)),
            dma((4,)),
        ]
        + [dma((peers,))] * 10
        + [dma((2, 2, 4)), dma((2, 2, 4)), dma, dma],
        compiler_params=pltpu.CompilerParams(
            collective_id=0, has_side_effects=True, vmem_limit_bytes=60 * 1024 * 1024
        ),
    )(
        band_pick,
        band_count,
        plan,
        pieces,
        tok_gain,
        trunk_gain.reshape(peers, cols),
        query_cot,
        resid_cot,
        bands_weight,
        query_weight,
    )
    return (queries, grads.reshape(bands, rows // bands, cols))


def solution(mesh):
    placed = (
        P("mp", None, None),
        P(),
        P(),
        P(None, "mp"),
        P(None, None, "mp"),
        P(),
        P(),
        P(None, "mp"),
        P("section", "mp"),
        P("section", "mp"),
    )
    return jax.shard_map(
        body,
        mesh=mesh,
        in_specs=placed,
        out_specs=(P("section", "mp"), P(None, "section", "mp")),
        check_vma=False,
    )
```

```python
import functools

import jax
import jax.numpy as jnp
from jax import lax
from jax.experimental import pallas as pl
from jax.experimental.pallas import tpu as pltpu
from jax.sharding import PartitionSpec as P

EPSILON = 1e-05
MESH = pl.DeviceIdType.MESH
F32 = jnp.float32
BF16 = jnp.bfloat16
NEAR = 8
TILE = 16
STEP = 112


def kernel(
    model_width,
    pick_ref,
    count_ref,
    plan_ref,
    pix_ref,
    gain_ref,
    tg_ref,
    qc_ref,
    rc_ref,
    w_hbm,
    wq_hbm,
    q_ref,
    bg_ref,
    live,
    member,
    w_ref,
    wq_ref,
    qc_rows,
    gain_wide,
    tg_wide,
    cand,
    xg,
    xt,
    stage,
    pre,
    crecv,
    p_ref,
    go,
    rows1,
    rows2,
    ps1,
    ps2,
    ag,
    tgng,
    gb,
    pb,
    cr,
    ybuf,
    yrecv,
    acc,
    local_sem,
    cand_send,
    cand_recv,
    x_send,
    x_recv,
    x_pass,
    pre_send,
    pre_recv,
    c_send,
    c_recv,
    p1_send,
    p1_recv,
    p2_send,
    p2_recv,
    ag_send,
    ag_recv,
    ag_pass,
    cr_send,
    cr_recv,
    y_send,
    y_recv,
):
    slots, groups = pick_ref.shape
    bands, tokens, patch = xg.shape
    cols = qc_ref.shape[0]
    peers = ag.shape[0]
    chips = peers // 2
    half_bands = bands // 2
    me = lax.axis_index("mp")
    chip = me // 2
    core = lax.rem(me, 2)
    twin = me + 1 - 2 * core
    section = lax.axis_index("section")
    half = section // NEAR
    ring = lax.rem(section, NEAR)
    low = lax.rem(section, 4)
    block = section // 4

    copy_wq = pltpu.make_async_copy(wq_hbm, wq_ref, local_sem.at[0])
    copy_w = pltpu.make_async_copy(w_hbm, w_ref, local_sem.at[1])
    copy_wq.start()
    copy_w.start()

    def peer(i):
        return lax.rem(me + i, peers)

    def near(i):
        return lax.rem(chip + i, chips)

    def at_ring(step):
        return half * NEAR + lax.rem(ring + step + NEAR, NEAR)

    down, up = at_ring(-1), at_ring(1)
    across = (1 - half) * NEAR + ring

    barrier = pltpu.get_barrier_semaphore()

    @pl.loop(1, peers)
    def _(i):
        pl.semaphore_signal(barrier, inc=1, device_id={"mp": peer(i)}, device_id_type=MESH)

    for other in (down, up, across):
        pl.semaphore_signal(barrier, inc=1, device_id={"section": other}, device_id_type=MESH)

    def remote(src, dst, send, recv, axis, to):
        return pltpu.make_async_remote_copy(
            src_ref=src,
            dst_ref=dst,
            send_sem=send,
            recv_sem=recv,
            device_id={axis: to},
            device_id_type=MESH,
        )

    @pl.loop(0, groups)
    def _(g):
        used = count_ref[g]
        for k in range(slots):
            live[g, k] = jnp.where(k < used, 1.0, 0.0).astype(F32)
        for b in range(bands):
            hit = jnp.float32(0.0)
            for k in range(slots):
                same = jnp.logical_and(pick_ref[k, g] == b, k < used)
                hit = hit + jnp.where(same, 1.0, 0.0).astype(F32)
            member[g, b] = hit

    qc_rows[...] = qc_ref[...].T
    pl.semaphore_wait(barrier, peers - 1 + 3)

    def piece(ref, j):
        start = pl.multiple_of((j // 2) * TILE, TILE)
        return ref.at[pl.ds(lax.rem(j, 2) * half_bands, half_bands), pl.ds(start, TILE), :]

    def cand_copy(i):
        to = peer(i)
        slot = me // 4
        return remote(
            piece(pix_ref, to), cand.at[slot], cand_send.at[i], cand_recv.at[slot], "mp", to
        )

    owner = lax.rem(me, 4) == low

    @pl.when(owner)
    def _():
        pltpu.make_async_copy(piece(pix_ref, me), cand.at[me // 4], cand_recv.at[me // 4]).start()

        @pl.loop(1, peers)
        def _(i):
            cand_copy(i).start()

    copy_wq.wait()

    def pre_copy(k):
        return remote(
            stage.at[2 * k + 1 - core], pre.at[k], pre_send.at[k], pre_recv.at[k], "mp", twin
        )

    @pl.loop(0, chips)
    def _(k):
        at = pl.ds(pl.multiple_of(k * 2 * cols, 128), 2 * cols)
        tiles = jnp.dot(qc_rows[...], wq_ref[:, at], preferred_element_type=F32).T
        stage[2 * k] = tiles[:cols].astype(BF16)
        stage[2 * k + 1] = tiles[cols:].astype(BF16)
        pre_copy(k).start()

    for c in range(4):
        pltpu.make_async_copy(cand.at[c], cand.at[c], cand_recv.at[c]).wait()

    def spread(view, send, recv):
        own = view(me)
        remote(own, own, send.at[0], recv.at[me], "mp", twin).start()

        @pl.loop(1, chips)
        def _(i):
            remote(own, own, send.at[i], recv.at[me], "mp", 2 * near(i) + core).start()

    def spread_wait(view, recv, hand):
        @pl.loop(1, chips)
        def _(i):
            src = 2 * near(i) + core
            block_of = view(src)
            pltpu.make_async_copy(block_of, block_of, recv.at[src]).wait()
            remote(block_of, block_of, hand.at[i], recv.at[src], "mp", twin).start()

        @pl.loop(0, chips)
        def _(i):
            src = 2 * near(i) + 1 - core
            block_of = view(src)
            pltpu.make_async_copy(block_of, block_of, recv.at[src]).wait()

    def spread_end(view, send, hand):
        own = view(me)

        @pl.loop(0, chips)
        def _(i):
            pltpu.make_async_copy(own, own, send.at[i]).wait()

        @pl.loop(1, chips)
        def _(i):
            pltpu.make_async_copy(own, own, hand.at[i]).wait()

    def x_view(j):
        return piece(xg, j)

    mine = pl.ds(pl.multiple_of(chip * TILE, TILE), TILE)
    xg[pl.ds(core * half_bands, half_bands), mine, :] = cand[plan_ref[block]]
    spread(x_view, x_send, x_recv)

    def cross_copy(i):
        k = near(i)
        return remote(
            stage.at[2 * k + core], crecv.at[chip], c_send.at[i], c_recv.at[chip], "mp", 2 * k + core
        )

    @pl.loop(1, chips)
    def _(i):
        k = near(i)
        pltpu.make_async_copy(pre.at[k], pre.at[k], pre_recv.at[k]).wait()
        stage[2 * k + core] = (stage[2 * k + core].astype(F32) + pre[k].astype(F32)).astype(BF16)
        cross_copy(i).start()

    pltpu.make_async_copy(pre.at[chip], pre.at[chip], pre_recv.at[chip]).wait()
    crecv[chip] = (stage[2 * chip + core].astype(F32) + pre[chip].astype(F32)).astype(BF16)

    gain_cols = gain_ref[...].T
    for g in range(groups):
        gain_wide[g] = jnp.broadcast_to(gain_cols[:, g : g + 1], (cols, tokens))
    tg_cols = tg_ref[...].T
    for k in range(tg_ref.shape[0]):
        tg_wide[128 * k : 128 * (k + 1), :] = jnp.broadcast_to(tg_cols[:, k : k + 1], (128, tokens))

    copy_w.wait()
    spread_wait(x_view, x_recv, x_pass)

    @pl.loop(0, bands)
    def _(b):
        p_ref[b] = lax.dot_general(
            w_ref[b], xg[b], (((1,), (1,)), ((), ())), preferred_element_type=F32
        )

    def fold(value):
        return jnp.sum(value.reshape(-1, 8, tokens), axis=0)

    def line(value):
        return jnp.sum(value, axis=0, keepdims=True)

    steps = range(0, cols, STEP)

    @pl.loop(0, groups)
    def _(g):
        square = jnp.zeros((8, tokens), F32)
        with_resid = jnp.zeros((8, tokens), F32)
        for d in steps:
            at = slice(d, d + STEP)
            out = live[g, 0] * p_ref[pick_ref[0, g], at, :]
            for k in range(1, slots):
                out = out + live[g, k] * p_ref[pick_ref[k, g], at, :]
            go[g, at, :] = out
            square = square + fold(out * out)
            with_resid = with_resid + fold(out * gain_wide[g, at, :] * rc_ref[at, :].astype(F32))
        rows1[pl.ds(g, 1), :] = line(square)
        rows1[pl.ds(groups + g, 1), :] = line(with_resid)

    def send_own(buf, send, recv):
        @pl.loop(1, peers)
        def _(i):
            remote(buf.at[me], buf.at[me], send.at[i], recv.at[me], "mp", peer(i)).start()

    def wait_recv(buf, recv):
        @pl.loop(1, peers)
        def _(i):
            src = peer(i)
            pltpu.make_async_copy(buf.at[src], buf.at[src], recv.at[src]).wait()

    def wait_send(buf, send):
        @pl.loop(1, peers)
        def _(i):
            pltpu.make_async_copy(buf.at[me], buf.at[me], send.at[i]).wait()

    def total(buf):
        value = buf[0]
        for i in range(1, peers):
            value = value + buf[i]
        return value

    ps1[me] = rows1[...]
    send_own(ps1, p1_send, p1_recv)

    @pl.loop(0, bands)
    def _(b):
        xt[b] = xg[b].T

    wait_recv(ps1, p1_recv)
    first = total(ps1)
    scale = lax.rsqrt(first[:groups] / model_width + EPSILON)

    for d in range(0, cols, 32):
        at = slice(d, d + 32)
        value = jnp.zeros((32, tokens), F32)
        for g in range(groups):
            value = value + go[g, at, :] * scale[g : g + 1, :] * gain_wide[g, at, :]
        ag[me, at, :] = value.astype(BF16)

    @pl.loop(1, chips)
    def _(i):
        k = near(i)
        pltpu.make_async_copy(crecv.at[k], crecv.at[k], c_recv.at[k]).wait()

    own_rows = pl.multiple_of(me * cols, 64)
    trunk_square = jnp.zeros((8, tokens), F32)
    trunk_grad = jnp.zeros((8, tokens), F32)
    for d in steps:
        at = slice(d, d + STEP)
        grad = crecv[0, at, :].astype(F32)
        for i in range(1, chips):
            grad = grad + crecv[i, at, :].astype(F32)
        grad = grad * tg_wide[pl.ds(own_rows + d, STEP), :]
        tgng[at, :] = grad
        trunk = ag[me, at, :].astype(F32)
        trunk_square = trunk_square + fold(trunk * trunk)
        trunk_grad = trunk_grad + fold(trunk * grad)
    rows2[2 * groups : 2 * groups + 1, :] = line(trunk_square)
    rows2[2 * groups + 1 : 2 * groups + 2, :] = line(trunk_grad)
    rows2[2 * groups + 2 :, :] = jnp.zeros((6, tokens), F32)

    @pl.loop(0, groups)
    def _(g):
        with_grad = jnp.zeros((8, tokens), F32)
        with_trunk = jnp.zeros((8, tokens), F32)
        for d in steps:
            at = slice(d, d + STEP)
            unit = go[g, at, :] * gain_wide[g, at, :]
            with_grad = with_grad + fold(unit * tgng[at, :])
            with_trunk = with_trunk + fold(unit * ag[me, at, :].astype(F32))
        rows2[pl.ds(g, 1), :] = line(with_grad)
        rows2[pl.ds(groups + g, 1), :] = line(with_trunk)

    ps2[me] = rows2[...]
    send_own(ps2, p2_send, p2_recv)

    def ag_view(j):
        return ag.at[j]

    spread(ag_view, ag_send, ag_recv)
    wait_recv(ps2, p2_recv)
    second = total(ps2)
    row_scale = lax.rsqrt(second[2 * groups : 2 * groups + 1] / model_width + EPSILON)
    row_stat = second[2 * groups + 1 : 2 * groups + 2] / model_width
    cube_stat = row_scale * row_scale * row_scale * row_stat
    group_stat = (
        first[groups : 2 * groups]
        + row_scale * second[:groups]
        - cube_stat * second[groups : 2 * groups]
    ) / model_width
    cube_group = scale * scale * scale * group_stat

    for d in range(0, cols, 32):
        at = slice(d, d + 32)
        grad = (
            rc_ref[at, :].astype(F32)
            + row_scale * tgng[at, :]
            - cube_stat * ag[me, at, :].astype(F32)
        )
        grad = grad.astype(BF16).astype(F32)
        for g in range(groups):
            go[g, at, :] = (
                scale[g : g + 1, :] * (grad * gain_wide[g, at, :])
                - go[g, at, :] * cube_group[g : g + 1, :]
            )

    @pl.loop(0, cols // 32)
    def _(r):
        at = pl.ds(pl.multiple_of(r * 32, 32), 32)
        for b0 in range(0, bands, 6):
            found = [jnp.zeros((32, tokens), F32) for _ in range(6)]
            for g in range(groups):
                value = go[g, at, :]
                found = [found[d] + member[g, b0 + d] * value for d in range(6)]
            for d in range(6):
                gb[b0 + d, at, :] = found[d].astype(BF16)

    @pl.loop(0, bands)
    def _(b):
        value = lax.dot_general(
            xt[b], gb[b], (((1,), (1,)), ((), ())), preferred_element_type=F32
        )
        rows = pl.ds(pl.multiple_of(b * TILE, TILE), TILE)
        pb[:, rows, :] = value.reshape(pb.shape[0], TILE, cols).astype(BF16)

    def unit(way, h, t):
        offset = (4 - t) if way else (t - 4)
        side = half if h else 1 - half
        return side * NEAR + lax.rem(ring + offset + NEAR, NEAR)

    def link(way, h, t):
        return remote(
            pb.at[unit(way, h, t)],
            cr.at[way, h, t],
            cr_send.at[way, h, t],
            cr_recv.at[way, h, t],
            "section",
            up if way else down,
        )

    for way, h, t in ((0, 0, 0), (1, 1, 0), (1, 0, 1), (0, 1, 1)):
        link(way, h, t).start()

    def advance(way, h, t):
        link(way, h, t - 1).wait_recv()
        at = unit(way, h, t)
        pb[at] = (pb[at].astype(F32) + cr[way, h, t - 1].astype(F32)).astype(BF16)
        link(way, h, t).start()

    advance(0, 0, 1)
    advance(1, 0, 2)
    advance(1, 1, 1)
    advance(0, 1, 2)

    spread_wait(ag_view, ag_recv, ag_pass)
    acc[...] = jnp.zeros_like(acc)

    @pl.loop(0, chips)
    def _(k):
        rows = pl.ds(pl.multiple_of(k * 2 * cols, 128), 2 * cols)
        trunk = ag[pl.ds(2 * k, 2)].reshape(2 * cols, tokens).astype(F32)
        normed = (trunk * row_scale * tg_wide[rows, :]).astype(BF16)
        acc[...] += jnp.dot(wq_ref[:, rows], normed, preferred_element_type=F32)

    q_ref[...] = acc[...].astype(BF16)

    advance(0, 0, 2)
    advance(1, 0, 3)
    advance(1, 1, 2)
    advance(0, 1, 3)
    advance(0, 0, 3)
    advance(1, 1, 3)

    def gathered(h):
        side = half if h else 1 - half
        link(1, h, 3).wait_recv()
        link(0, h, 3).wait_recv()
        return (
            pb[side * NEAR + ring].astype(F32) + cr[0, h, 3].astype(F32) + cr[1, h, 3].astype(F32)
        )

    ybuf[...] = gathered(0).astype(BF16)
    over = remote(ybuf, yrecv, y_send, y_recv, "section", across)
    over.start()
    own_sum = gathered(1)
    over.wait_recv()
    bg_ref[...] = (own_sum + yrecv[...].astype(F32)).astype(BF16)

    over.wait_send()
    for way, h, t0 in ((0, 0, 0), (1, 1, 0), (0, 1, 1), (1, 0, 1)):
        for t in range(t0, 4):
            link(way, h, t).wait_send()

    @pl.when(owner)
    def _():
        @pl.loop(1, peers)
        def _(i):
            cand_copy(i).wait_send()

    spread_end(x_view, x_send, x_pass)
    spread_end(ag_view, ag_send, ag_pass)

    @pl.loop(0, chips)
    def _(k):
        pre_copy(k).wait_send()

    @pl.loop(1, chips)
    def _(i):
        cross_copy(i).wait_send()

    wait_send(ps1, p1_send)
    wait_send(ps2, p2_send)


def body(
    pixels,
    band_pick,
    band_count,
    tok_gain,
    bands_weight,
    plan,
    trunk_gain,
    query_weight,
    query_cot,
    resid_cot,
):
    peers = lax.axis_size("mp")
    chips = peers // 2
    sections = lax.axis_size("section")
    groups = band_pick.shape[0]
    tokens, bands, patch = pixels.shape
    cols = bands_weight.shape[2]
    model_width = cols * peers
    rows = bands * patch // sections
    vmem = pl.BlockSpec(memory_space=pltpu.VMEM)
    smem = pl.BlockSpec(memory_space=pltpu.SMEM)
    hbm = pl.BlockSpec(memory_space=pl.ANY)
    dma = pltpu.SemaphoreType.DMA
    queries, grads = pl.pallas_call(
        functools.partial(kernel, model_width),
        out_shape=(
            jax.ShapeDtypeStruct((cols, tokens), BF16),
            jax.ShapeDtypeStruct((rows, cols), BF16),
        ),
        in_specs=[smem] * 3 + [vmem] * 5 + [hbm] * 2,
        out_specs=(vmem, vmem),
        scratch_shapes=[
            pltpu.SMEM((groups, band_pick.shape[1]), F32),
            pltpu.SMEM((groups, bands), F32),
            pltpu.VMEM((bands, cols, patch), BF16),
            pltpu.VMEM((cols, model_width), BF16),
            pltpu.VMEM((tokens, cols), BF16),
            pltpu.VMEM((groups, cols, tokens), F32),
            pltpu.VMEM((model_width, tokens), F32),
            pltpu.VMEM((4, bands // 2, TILE, patch), BF16),
            pltpu.VMEM((bands, tokens, patch), BF16),
            pltpu.VMEM((bands, patch, tokens), BF16),
            pltpu.VMEM((peers, cols, tokens), BF16),
            pltpu.VMEM((chips, cols, tokens), BF16),
            pltpu.VMEM((chips, cols, tokens), BF16),
            pltpu.VMEM((bands, cols, tokens), F32),
            pltpu.VMEM((groups, cols, tokens), F32),
            pltpu.VMEM((2 * groups, tokens), F32),
            pltpu.VMEM((2 * groups + 8, tokens), F32),
            pltpu.VMEM((peers, 2 * groups, tokens), F32),
            pltpu.VMEM((peers, 2 * groups + 8, tokens), F32),
            pltpu.VMEM((peers, cols, tokens), BF16),
            pltpu.VMEM((cols, tokens), F32),
            pltpu.VMEM((bands, cols, tokens), BF16),
            pltpu.VMEM((sections, rows, cols), BF16),
            pltpu.VMEM((2, 2, 4, rows, cols), BF16),
            pltpu.VMEM((rows, cols), BF16),
            pltpu.VMEM((rows, cols), BF16),
            pltpu.VMEM((cols, tokens), F32),
            dma((2,)),
            dma((peers,)),
            dma((4,)),
            dma((chips,)),
            dma((peers,)),
            dma((chips,)),
            dma((chips,)),
            dma((chips,)),
            dma((chips,)),
            dma((chips,)),
            dma((peers,)),
            dma((peers,)),
            dma((peers,)),
            dma((peers,)),
            dma((chips,)),
            dma((peers,)),
            dma((chips,)),
            dma((2, 2, 4)),
            dma((2, 2, 4)),
            dma,
            dma,
        ],
        compiler_params=pltpu.CompilerParams(
            collective_id=0, has_side_effects=True, vmem_limit_bytes=60 * 1024 * 1024
        ),
    )(
        band_pick.T,
        band_count,
        plan,
        pixels.transpose(1, 0, 2),
        tok_gain,
        trunk_gain.reshape(-1, 128),
        query_cot.T,
        resid_cot.T,
        bands_weight.transpose(0, 2, 1),
        query_weight.T,
    )
    return (queries.T, grads.reshape(bands, rows // bands, cols))


def solution(mesh):
    placed = (
        P("mp", None, None),
        P(),
        P(),
        P(None, "mp"),
        P(None, None, "mp"),
        P(),
        P(),
        P(None, "mp"),
        P("section", "mp"),
        P("section", "mp"),
    )
    return jax.shard_map(
        body,
        mesh=mesh,
        in_specs=placed,
        out_specs=(P("section", "mp"), P(None, "section", "mp")),
        check_vma=False,
    )
```

```python
import functools

import jax
import jax.numpy as jnp
from jax import lax
from jax.experimental import pallas as pl
from jax.experimental.pallas import tpu as pltpu
from jax.sharding import PartitionSpec as P

EPSILON = 1e-05
MESH = pl.DeviceIdType.MESH
F32 = jnp.float32
BF16 = jnp.bfloat16
NEAR = 8
TILE = 16
STEP = 112


def kernel(
    model_width,
    pick_ref,
    count_ref,
    plan_ref,
    pix_ref,
    gain_ref,
    tg_ref,
    qc_ref,
    rc_ref,
    w_hbm,
    wq_hbm,
    q_ref,
    bg_ref,
    live,
    member,
    w_ref,
    wq_ref,
    qc_rows,
    gain_wide,
    tg_wide,
    cand,
    xg,
    xt,
    stage,
    pre,
    crecv,
    p_ref,
    go,
    rows1,
    rows2,
    rows3,
    twin1,
    twin2,
    twin3,
    ps1,
    ps2,
    ps3,
    ag,
    tgng,
    gb,
    pb,
    cr,
    ybuf,
    yrecv,
    acc,
    local_sem,
    cand_send,
    cand_recv,
    x_send,
    x_recv,
    x_pass,
    pre_send,
    pre_recv,
    c_send,
    c_recv,
    p1_send,
    p1_recv,
    p2_send,
    p2_recv,
    p3_send,
    p3_recv,
    twin_send,
    twin_recv,
    ag_send,
    ag_recv,
    ag_pass,
    cr_send,
    cr_recv,
    y_send,
    y_recv,
):
    slots, groups = pick_ref.shape
    bands, tokens, patch = xg.shape
    cols = qc_ref.shape[0]
    peers = ag.shape[0]
    chips = peers // 2
    half_bands = bands // 2
    me = lax.axis_index("mp")
    chip = me // 2
    core = lax.rem(me, 2)
    twin = me + 1 - 2 * core
    section = lax.axis_index("section")
    half = section // NEAR
    ring = lax.rem(section, NEAR)
    low = lax.rem(section, 4)
    block = section // 4

    copy_wq = pltpu.make_async_copy(wq_hbm, wq_ref, local_sem.at[0])
    copy_w = pltpu.make_async_copy(w_hbm, w_ref, local_sem.at[1])
    copy_wq.start()
    copy_w.start()

    def peer(i):
        return lax.rem(me + i, peers)

    def near(i):
        return lax.rem(chip + i, chips)

    def at_ring(step):
        return half * NEAR + lax.rem(ring + step + NEAR, NEAR)

    down, up = at_ring(-1), at_ring(1)
    across = (1 - half) * NEAR + ring

    barrier = pltpu.get_barrier_semaphore()

    @pl.loop(1, peers)
    def _(i):
        pl.semaphore_signal(barrier, inc=1, device_id={"mp": peer(i)}, device_id_type=MESH)

    for other in (down, up, across):
        pl.semaphore_signal(barrier, inc=1, device_id={"section": other}, device_id_type=MESH)

    def remote(src, dst, send, recv, axis, to):
        return pltpu.make_async_remote_copy(
            src_ref=src,
            dst_ref=dst,
            send_sem=send,
            recv_sem=recv,
            device_id={axis: to},
            device_id_type=MESH,
        )

    @pl.loop(0, groups)
    def _(g):
        used = count_ref[g]
        for k in range(slots):
            live[g, k] = jnp.where(k < used, 1.0, 0.0).astype(F32)
        for b in range(bands):
            hit = jnp.float32(0.0)
            for k in range(slots):
                same = jnp.logical_and(pick_ref[k, g] == b, k < used)
                hit = hit + jnp.where(same, 1.0, 0.0).astype(F32)
            member[g, b] = hit

    qc_rows[...] = qc_ref[...].T

    copy_wq.wait()

    @pl.loop(0, chips)
    def _(k):
        at = pl.ds(pl.multiple_of(k * 2 * cols, 128), 2 * cols)
        tiles = jnp.dot(qc_rows[...], wq_ref[:, at], preferred_element_type=F32).T
        stage[2 * k] = tiles[:cols].astype(BF16)
        stage[2 * k + 1] = tiles[cols:].astype(BF16)

    pl.semaphore_wait(barrier, peers - 1 + 3)

    def piece(ref, j):
        start = pl.multiple_of((j // 2) * TILE, TILE)
        return ref.at[pl.ds(lax.rem(j, 2) * half_bands, half_bands), pl.ds(start, TILE), :]

    def cand_copy(i):
        to = peer(i)
        slot = me // 4
        return remote(
            piece(pix_ref, to), cand.at[slot], cand_send.at[i], cand_recv.at[slot], "mp", to
        )

    owner = lax.rem(me, 4) == low

    @pl.when(owner)
    def _():
        pltpu.make_async_copy(piece(pix_ref, me), cand.at[me // 4], cand_recv.at[me // 4]).start()

        @pl.loop(1, peers)
        def _(i):
            cand_copy(i).start()

    def pre_copy(k):
        return remote(
            stage.at[2 * k + 1 - core], pre.at[k], pre_send.at[k], pre_recv.at[k], "mp", twin
        )

    @pl.loop(1, chips)
    def _(i):
        pre_copy(near(i)).start()

    pre_copy(chip).start()

    gain_cols = gain_ref[...].T
    for g in range(groups):
        gain_wide[g] = jnp.broadcast_to(gain_cols[:, g : g + 1], (cols, tokens))

    def cross_copy(i):
        k = near(i)
        return remote(
            stage.at[2 * k + core], crecv.at[chip], c_send.at[i], c_recv.at[chip], "mp", 2 * k + core
        )

    def cross_out(i):
        k = near(i)
        pltpu.make_async_copy(pre.at[k], pre.at[k], pre_recv.at[k]).wait()
        stage[2 * k + core] = (stage[2 * k + core].astype(F32) + pre[k].astype(F32)).astype(BF16)
        cross_copy(i).start()

    early = 3

    @pl.loop(1, early)
    def _(i):
        cross_out(i)

    for c in range(4):
        pltpu.make_async_copy(cand.at[c], cand.at[c], cand_recv.at[c]).wait()

    def spread(view, send, recv):
        own = view(me)
        remote(own, own, send.at[0], recv.at[me], "mp", twin).start()

        @pl.loop(1, chips)
        def _(i):
            remote(own, own, send.at[i], recv.at[me], "mp", 2 * near(i) + core).start()

    def spread_wait(view, recv, hand):
        @pl.loop(1, chips)
        def _(i):
            src = 2 * near(i) + core
            block_of = view(src)
            pltpu.make_async_copy(block_of, block_of, recv.at[src]).wait()
            remote(block_of, block_of, hand.at[i], recv.at[src], "mp", twin).start()

        @pl.loop(0, chips)
        def _(i):
            src = 2 * near(i) + 1 - core
            block_of = view(src)
            pltpu.make_async_copy(block_of, block_of, recv.at[src]).wait()

    def spread_end(view, send, hand):
        own = view(me)

        @pl.loop(0, chips)
        def _(i):
            pltpu.make_async_copy(own, own, send.at[i]).wait()

        @pl.loop(1, chips)
        def _(i):
            pltpu.make_async_copy(own, own, hand.at[i]).wait()

    def x_view(j):
        return piece(xg, j)

    mine = pl.ds(pl.multiple_of(chip * TILE, TILE), TILE)
    xg[pl.ds(core * half_bands, half_bands), mine, :] = cand[plan_ref[block]]
    spread(x_view, x_send, x_recv)

    @pl.loop(early, chips)
    def _(i):
        cross_out(i)

    pltpu.make_async_copy(pre.at[chip], pre.at[chip], pre_recv.at[chip]).wait()
    crecv[chip] = (stage[2 * chip + core].astype(F32) + pre[chip].astype(F32)).astype(BF16)

    tg_cols = tg_ref[...].T
    for k in range(tg_ref.shape[0]):
        tg_wide[128 * k : 128 * (k + 1), :] = jnp.broadcast_to(tg_cols[:, k : k + 1], (128, tokens))

    copy_w.wait()
    spread_wait(x_view, x_recv, x_pass)

    @pl.loop(0, bands)
    def _(b):
        p_ref[b] = lax.dot_general(
            w_ref[b], xg[b], (((1,), (1,)), ((), ())), preferred_element_type=F32
        )

    def fold(value):
        return jnp.sum(value.reshape(-1, 8, tokens), axis=0)

    def line(value):
        return jnp.sum(value, axis=0, keepdims=True)

    steps = range(0, cols, STEP)

    @pl.loop(0, groups)
    def _(g):
        square = jnp.zeros((8, tokens), F32)
        for d in steps:
            at = slice(d, d + STEP)
            out = live[g, 0] * p_ref[pick_ref[0, g], at, :]
            for k in range(1, slots):
                out = out + live[g, k] * p_ref[pick_ref[k, g], at, :]
            go[g, at, :] = out
            square = square + fold(out * out)
        rows1[pl.ds(g, 1), :] = line(square)

    def twin_copy(n, rows, there):
        return remote(rows, there, twin_send.at[n], twin_recv.at[n], "mp", twin)

    def chip_copy(buf, send, recv, i):
        return remote(
            buf.at[chip], buf.at[chip], send.at[i], recv.at[chip], "mp", 2 * near(i) + core
        )

    def to_chips(n, rows, there, buf, send, recv):
        twin_copy(n, rows, there).wait_recv()
        buf[chip] = rows[...] + there[...]

        @pl.loop(1, chips)
        def _(i):
            chip_copy(buf, send, recv, i).start()

    def total(buf, recv):
        @pl.loop(1, chips)
        def _(i):
            k = near(i)
            pltpu.make_async_copy(buf.at[k], buf.at[k], recv.at[k]).wait()

        value = buf[0]
        for i in range(1, chips):
            value = value + buf[i]
        return value

    def sum_end(n, rows, there, buf, send, recv):
        twin_copy(n, rows, there).wait_send()

        @pl.loop(1, chips)
        def _(i):
            chip_copy(buf, send, recv, i).wait_send()

    sum1 = (0, rows1, twin1, ps1, p1_send, p1_recv)
    sum2 = (1, rows2, twin2, ps2, p2_send, p2_recv)
    sum3 = (2, rows3, twin3, ps3, p3_send, p3_recv)

    twin_copy(0, rows1, twin1).start()

    @pl.loop(0, bands // 2)
    def _(b):
        xt[b] = xg[b].T

    to_chips(*sum1)

    @pl.loop(bands // 2, bands)
    def _(b):
        xt[b] = xg[b].T

    @pl.loop(1, chips)
    def _(i):
        k = near(i)
        pltpu.make_async_copy(crecv.at[k], crecv.at[k], c_recv.at[k]).wait()

    own_rows = pl.multiple_of(me * cols, 64)
    for d in steps:
        at = slice(d, d + STEP)
        grad = crecv[0, at, :].astype(F32)
        for i in range(1, chips):
            grad = grad + crecv[i, at, :].astype(F32)
        tgng[at, :] = grad * tg_wide[pl.ds(own_rows + d, STEP), :]

    @pl.loop(0, groups)
    def _(g):
        with_resid = jnp.zeros((8, tokens), F32)
        with_grad = jnp.zeros((8, tokens), F32)
        for d in steps:
            at = slice(d, d + STEP)
            unit = go[g, at, :] * gain_wide[g, at, :]
            with_resid = with_resid + fold(unit * rc_ref[at, :].astype(F32))
            with_grad = with_grad + fold(unit * tgng[at, :])
        rows2[pl.ds(g, 1), :] = line(with_resid)
        rows2[pl.ds(groups + g, 1), :] = line(with_grad)

    twin_copy(1, rows2, twin2).start()
    scale = lax.rsqrt(total(ps1, p1_recv) / model_width + EPSILON)

    trunk_square = jnp.zeros((8, tokens), F32)
    trunk_grad = jnp.zeros((8, tokens), F32)
    for d in range(0, cols, 32):
        at = slice(d, d + 32)
        value = jnp.zeros((32, tokens), F32)
        for g in range(groups):
            value = value + go[g, at, :] * scale[g : g + 1, :] * gain_wide[g, at, :]
        low_value = value.astype(BF16)
        ag[me, at, :] = low_value
        trunk = low_value.astype(F32)
        trunk_square = trunk_square + fold(trunk * trunk)
        trunk_grad = trunk_grad + fold(trunk * tgng[at, :])
    rows3[groups : groups + 1, :] = line(trunk_square)
    rows3[groups + 1 : groups + 2, :] = line(trunk_grad)
    rows3[groups + 2 :, :] = jnp.zeros((6, tokens), F32)

    @pl.loop(0, groups)
    def _(g):
        with_trunk = jnp.zeros((8, tokens), F32)
        for d in steps:
            at = slice(d, d + STEP)
            unit = go[g, at, :] * gain_wide[g, at, :]
            with_trunk = with_trunk + fold(unit * ag[me, at, :].astype(F32))
        rows3[pl.ds(g, 1), :] = line(with_trunk)

    twin_copy(2, rows3, twin3).start()
    to_chips(*sum2)
    to_chips(*sum3)

    def ag_view(j):
        return ag.at[j]

    spread(ag_view, ag_send, ag_recv)
    second = total(ps2, p2_recv)
    third = total(ps3, p3_recv)
    row_scale = lax.rsqrt(third[groups : groups + 1] / model_width + EPSILON)
    row_stat = third[groups + 1 : groups + 2] / model_width
    cube_stat = row_scale * row_scale * row_scale * row_stat
    group_stat = (
        second[:groups] + row_scale * second[groups:] - cube_stat * third[:groups]
    ) / model_width
    cube_group = scale * scale * scale * group_stat

    for d in range(0, cols, 32):
        at = slice(d, d + 32)
        grad = (
            rc_ref[at, :].astype(F32)
            + row_scale * tgng[at, :]
            - cube_stat * ag[me, at, :].astype(F32)
        )
        grad = grad.astype(BF16).astype(F32)
        for g in range(groups):
            go[g, at, :] = (
                scale[g : g + 1, :] * (grad * gain_wide[g, at, :])
                - go[g, at, :] * cube_group[g : g + 1, :]
            )

    def unit(way, h, t):
        offset = (4 - t) if way else (t - 4)
        side = half if h else 1 - half
        return side * NEAR + lax.rem(ring + offset + NEAR, NEAR)

    def link(way, h, j, t):
        return remote(
            pb.at[unit(way, h, t), j],
            cr.at[way, h, j, t],
            cr_send.at[way, h, j, t],
            cr_recv.at[way, h, j, t],
            "section",
            up if way else down,
        )

    def first_step(way, h):
        return 0 if way == h else 1

    def begin(h, j):
        for way in range(2):
            link(way, h, j, first_step(way, h)).start()

    def advance(h, j, n):
        for way in range(2):
            t = first_step(way, h) + n
            if t < 4:
                link(way, h, j, t - 1).wait_recv()
                at = unit(way, h, t)
                pb[at, j] = (pb[at, j].astype(F32) + cr[way, h, j, t - 1].astype(F32)).astype(BF16)
                link(way, h, j, t).start()

    def gathered(h, j):
        side = half if h else 1 - half
        link(0, h, j, 3).wait_recv()
        link(1, h, j, 3).wait_recv()
        return (
            pb[side * NEAR + ring, j].astype(F32)
            + cr[0, h, j, 3].astype(F32)
            + cr[1, h, j, 3].astype(F32)
        )

    def over(j):
        return remote(ybuf.at[j], yrecv.at[j], y_send.at[j], y_recv.at[j], "section", across)

    for j in range(2):

        @pl.loop(0, cols // 32)
        def _(r):
            at = pl.ds(pl.multiple_of(r * 32, 32), 32)
            found = [jnp.zeros((32, tokens), F32) for _ in range(half_bands)]
            for g in range(groups):
                value = go[g, at, :]
                found = [
                    found[d] + member[g, half_bands * j + d] * value for d in range(half_bands)
                ]
            for d in range(half_bands):
                gb[d, at, :] = found[d].astype(BF16)

        @pl.loop(0, half_bands // 2)
        def _(n):
            rests = []
            for e in range(2):
                value = lax.dot_general(
                    xt[half_bands * j + 2 * n + e],
                    gb[2 * n + e],
                    (((1,), (1,)), ((), ())),
                    preferred_element_type=F32,
                )
                value = value.reshape(pb.shape[0], TILE, cols)
                for c in range(3):
                    rows = pl.ds(pl.multiple_of((6 * n + 3 * e + c) * TILE, TILE), TILE)
                    pb[:, j, rows, :] = value[:, :, 128 * c : 128 * (c + 1)].astype(BF16)
                rests.append(value[:, :, 384:])
            rows = pl.ds(pl.multiple_of((3 * half_bands + n) * TILE, TILE), TILE)
            pb[:, j, rows, :] = jnp.concatenate(rests, axis=2).astype(BF16)

        begin(0, j)

    advance(0, 0, 1)
    advance(0, 1, 1)
    begin(1, 0)
    advance(0, 0, 2)
    advance(0, 1, 2)
    begin(1, 1)
    spread_wait(ag_view, ag_recv, ag_pass)
    advance(0, 0, 3)
    advance(0, 1, 3)
    advance(1, 0, 1)
    advance(1, 1, 1)
    for j in range(2):
        ybuf[j] = gathered(0, j).astype(BF16)
        over(j).start()
    for n in (2, 3):
        for j in range(2):
            advance(1, j, n)

    acc[...] = jnp.zeros_like(acc)

    @pl.loop(0, chips)
    def _(k):
        rows = pl.ds(pl.multiple_of(k * 2 * cols, 128), 2 * cols)
        trunk = ag[pl.ds(2 * k, 2)].reshape(2 * cols, tokens).astype(F32)
        normed = (trunk * row_scale * tg_wide[rows, :]).astype(BF16)
        acc[...] += jnp.dot(wq_ref[:, rows], normed, preferred_element_type=F32)

    q_ref[...] = acc[...].astype(BF16)
    for j in range(2):
        own_sum = gathered(1, j)
        over(j).wait_recv()
        bg_ref[j] = (own_sum + yrecv[j].astype(F32)).astype(BF16)

    for j in range(2):
        over(j).wait_send()
        for h in range(2):
            for way in range(2):
                for t in range(first_step(way, h), 4):
                    link(way, h, j, t).wait_send()

    @pl.when(owner)
    def _():
        @pl.loop(1, peers)
        def _(i):
            cand_copy(i).wait_send()

    spread_end(x_view, x_send, x_pass)
    spread_end(ag_view, ag_send, ag_pass)

    @pl.loop(0, chips)
    def _(k):
        pre_copy(k).wait_send()

    @pl.loop(1, chips)
    def _(i):
        cross_copy(i).wait_send()

    for each in (sum1, sum2, sum3):
        sum_end(*each)


def place(bands, q_ref, bg_ref, q_out, bg_out):
    half_bands = bands // 2
    q_out[...] = q_ref[...]
    for b in range(bands):
        j, d = b // half_bands, b % half_bands
        for c in range(3):
            rows = (3 * d + c) * TILE
            bg_out[b, :, 128 * c : 128 * (c + 1)] = bg_ref[j, rows : rows + TILE, :]
        rows = (3 * half_bands + d // 2) * TILE
        side = 64 * (d % 2)
        bg_out[b, :, 384:] = bg_ref[j, rows : rows + TILE, side : side + 64]


def body(
    pixels,
    band_pick,
    band_count,
    tok_gain,
    bands_weight,
    plan,
    trunk_gain,
    query_weight,
    query_cot,
    resid_cot,
):
    peers = lax.axis_size("mp")
    chips = peers // 2
    sections = lax.axis_size("section")
    groups = band_pick.shape[0]
    tokens, bands, patch = pixels.shape
    cols = bands_weight.shape[2]
    model_width = cols * peers
    rows = bands * patch // sections
    packed = (2, rows * cols // 256, 128)
    vmem = pl.BlockSpec(memory_space=pltpu.VMEM)
    smem = pl.BlockSpec(memory_space=pltpu.SMEM)
    hbm = pl.BlockSpec(memory_space=pl.ANY)
    dma = pltpu.SemaphoreType.DMA
    queries, grads = pl.pallas_call(
        functools.partial(kernel, model_width),
        out_shape=(
            jax.ShapeDtypeStruct((cols, tokens), BF16),
            jax.ShapeDtypeStruct(packed, BF16),
        ),
        in_specs=[smem] * 3 + [hbm] + [vmem] * 4 + [hbm] * 2,
        out_specs=(vmem, vmem),
        scratch_shapes=[
            pltpu.SMEM((groups, band_pick.shape[1]), F32),
            pltpu.SMEM((groups, bands), F32),
            pltpu.VMEM((bands, cols, patch), BF16),
            pltpu.VMEM((cols, model_width), BF16),
            pltpu.VMEM((tokens, cols), BF16),
            pltpu.VMEM((groups, cols, tokens), F32),
            pltpu.VMEM((model_width, tokens), F32),
            pltpu.VMEM((4, bands // 2, TILE, patch), BF16),
            pltpu.VMEM((bands, tokens, patch), BF16),
            pltpu.VMEM((bands, patch, tokens), BF16),
            pltpu.VMEM((peers, cols, tokens), BF16),
            pltpu.VMEM((chips, cols, tokens), BF16),
            pltpu.VMEM((chips, cols, tokens), BF16),
            pltpu.VMEM((bands, cols, tokens), F32),
            pltpu.VMEM((groups, cols, tokens), F32),
            pltpu.VMEM((groups, tokens), F32),
            pltpu.VMEM((2 * groups, tokens), F32),
            pltpu.VMEM((groups + 8, tokens), F32),
            pltpu.VMEM((groups, tokens), F32),
            pltpu.VMEM((2 * groups, tokens), F32),
            pltpu.VMEM((groups + 8, tokens), F32),
            pltpu.VMEM((chips, groups, tokens), F32),
            pltpu.VMEM((chips, 2 * groups, tokens), F32),
            pltpu.VMEM((chips, groups + 8, tokens), F32),
            pltpu.VMEM((peers, cols, tokens), BF16),
            pltpu.VMEM((cols, tokens), F32),
            pltpu.VMEM((bands // 2, cols, tokens), BF16),
            pltpu.VMEM((sections,) + packed, BF16),
            pltpu.VMEM((2, 2, 2, 4) + packed[1:], BF16),
            pltpu.VMEM(packed, BF16),
            pltpu.VMEM(packed, BF16),
            pltpu.VMEM((cols, tokens), F32),
            dma((2,)),
            dma((peers,)),
            dma((4,)),
            dma((chips,)),
            dma((peers,)),
            dma((chips,)),
            dma((chips,)),
            dma((chips,)),
            dma((chips,)),
            dma((chips,)),
            dma((chips,)),
            dma((chips,)),
            dma((chips,)),
            dma((chips,)),
            dma((chips,)),
            dma((chips,)),
            dma((3,)),
            dma((3,)),
            dma((chips,)),
            dma((peers,)),
            dma((chips,)),
            dma((2, 2, 2, 4)),
            dma((2, 2, 2, 4)),
            dma((2,)),
            dma((2,)),
        ],
        compiler_params=pltpu.CompilerParams(
            collective_id=0, has_side_effects=True, vmem_limit_bytes=60 * 1024 * 1024
        ),
    )(
        band_pick.T,
        band_count,
        plan,
        pixels.transpose(1, 0, 2),
        tok_gain,
        trunk_gain.reshape(-1, 128),
        query_cot.T,
        resid_cot.T,
        bands_weight.transpose(0, 2, 1),
        query_weight.T,
    )
    queries, grads = pl.pallas_call(
        functools.partial(place, bands),
        out_shape=(
            jax.ShapeDtypeStruct((cols, tokens), BF16),
            jax.ShapeDtypeStruct((bands, rows // bands, cols), BF16),
        ),
        in_specs=[vmem] * 2,
        out_specs=(vmem, vmem),
    )(queries, grads)
    return (queries.T, grads)


def solution(mesh):
    placed = (
        P("mp", None, None),
        P(),
        P(),
        P(None, "mp"),
        P(None, None, "mp"),
        P(),
        P(),
        P(None, "mp"),
        P("section", "mp"),
        P("section", "mp"),
    )
    return jax.shard_map(
        body,
        mesh=mesh,
        in_specs=placed,
        out_specs=(P("section", "mp"), P(None, "section", "mp")),
        check_vma=False,
    )
```
